32 devices in a mesh: wave: 2 (over y), ty: 4 (over z), tx: 4 (over x, core).
Axes of the slice: x: 2, y: 2, z: 4, core: 2. Of those that a mesh axis runs over, the one named last changes fastest.
Arguments:
- object_field: float32 [2, 2048, 2048], P(None, 'ty', 'tx'), may hold values from -5 to 5
- probes: float32 [2, 2, 256, 256], P('wave'), may hold values from -5 to 5
- measured: float32 [4, 4, 8, 256, 256], P('ty', 'tx'), may hold values from 0.1 to 4
- positions: int32 [4, 4, 8, 2], P('ty', 'tx'), may hold values from 0 to 256, as said below
- weights: float32 [2], P('wave'), may hold values from 0.5 to 12, as said below
Outputs:
- new_object: float32 [2, 2048, 2048], P(None, 'ty', 'tx')
- new_probes: float32 [2, 2, 256, 256], P('wave')
The draws below stay inside these ranges and needn't reach their ends.
Inputs may be any that keep to these rules, and one draw needn't show every extreme that they name: `positions`: each frame lies wholly inside its tile; some offset equals 0 and some equals 256. Positive weights.
All inputs are finite; a program needn't handle non-finite values.
Results may differ from the reference program's by a relative error of at most 0.0003.
Values sent between devices are 32-bit elements; how exact they have to be, the bound alone decides.
A program may use at most 64 MiB of HBM per device.

```python
import math
import jax
import jax.numpy as jnp
from jax import lax

P_SIZE = 256
TILE = 512
FRAMES = 8
WAVES = 2
ROWS_T = 4
COLS_T = 4
NY = 2048
NX = 2048


def draw_positions(key, part):
    first, second, third = jax.random.split(jax.random.fold_in(key, 17), 3)
    total = ROWS_T * COLS_T * FRAMES * 2
    flat = jax.random.randint(first, (total,), 0, TILE - P_SIZE + 1)
    lowest = jax.random.randint(second, (), 0, total)
    stride = jax.random.randint(third, (), 1, total)
    highest_at = (lowest + stride) % total
    flat = flat.at[lowest].set(0)
    flat = flat.at[highest_at].set(TILE - P_SIZE)
    return flat.reshape(ROWS_T, COLS_T, FRAMES, 2).astype(jnp.int32)


def draw_weights(key, part):
    ramp = 1.0 + 2.0 * jnp.arange(WAVES, dtype=jnp.float32) / max(WAVES - 1, 1)
    jitter = jax.random.uniform(jax.random.fold_in(key, 29), (WAVES,), jnp.float32, 0.7, 1.3)
    values = ramp * jitter
    return values.astype(jnp.float32)


def level_of(own_key, extent, pieces, low, high):
    factor_of, own = 1.0, jax.random.fold_in(own_key, 6)
    for position, parts in pieces:
        steps = jnp.exp(jax.random.uniform(jax.random.fold_in(own, position), (parts,), jnp.float32, low / len(pieces), high / len(pieces)))
        factor_of = factor_of * jnp.repeat(steps, extent[position] // parts).reshape([-1 if axis == position else 1 for axis in range(len(extent))])
    return factor_of


def noise(rng, extent, spread, bound, cuts=(), held_as=jnp.bfloat16):
    entries = spread * jax.random.normal(rng, extent, jnp.float32)
    if cuts:
        entries = entries * level_of(rng, extent, cuts, -0.22, 0.18)
    return jnp.clip(entries, -bound, bound).astype(held_as)


def setup_inputs(seed: int = 0) -> dict:
    arg_keys = jax.random.split(jax.random.key(seed), 6)
    return {
        "object_field": noise(arg_keys[0], (2, NY, NX), 0.7, 5.0, ((1, 4), (2, 4)), jnp.float32),
        "probes": noise(arg_keys[1], (WAVES, 2, P_SIZE, P_SIZE), 0.7, 5.0, ((0, 2),), jnp.float32),
        "measured": jnp.clip(jnp.exp(math.log(4.0) - 3.6888794 * jax.random.uniform(arg_keys[2], (ROWS_T, COLS_T, FRAMES, P_SIZE, P_SIZE), jnp.float32) ** level_of(arg_keys[2], (ROWS_T, COLS_T, FRAMES, P_SIZE, P_SIZE), ((0, 4), (1, 4)), -0.2, 0.2)), 0.1, 4.0),
        "positions": draw_positions(jax.random.fold_in(arg_keys[5], 71), 0),
        "weights": draw_weights(jax.random.fold_in(arg_keys[5], 71), 0),
    }


highest = lax.Precision.HIGHEST
damping = 1.0
intensity_offset = 0.1

def tables(length):
    indices = jnp.arange(length, dtype=jnp.int32)
    product = indices[:, None] * indices[None, :] % length
    angles = 2.0 * math.pi / length * product.astype(jnp.float32)
    norm_scale = 1.0 / math.sqrt(length)
    return (jnp.cos(angles) * norm_scale, -jnp.sin(angles) * norm_scale)

def transform(real_part, imag_part, cosine_table, sine_table):
    left_real = jnp.matmul(cosine_table, real_part, precision=highest) - jnp.matmul(sine_table, imag_part, precision=highest)
    left_imag = jnp.matmul(cosine_table, imag_part, precision=highest) + jnp.matmul(sine_table, real_part, precision=highest)
    out_real = jnp.matmul(left_real, cosine_table, precision=highest) - jnp.matmul(left_imag, sine_table, precision=highest)
    out_imag = jnp.matmul(left_real, sine_table, precision=highest) + jnp.matmul(left_imag, cosine_table, precision=highest)
    return (out_real, out_imag)

def tile_update(tile_field, probe_real, probe_imag, illumination, measured_tile, offsets, weights, total_weight, cosine_table, sine_table):
    anchor = jnp.zeros((), jnp.int32)
    patches = jnp.stack([lax.dynamic_slice(tile_field, (anchor, offsets[frame_idx, 0], offsets[frame_idx, 1]), (2, P_SIZE, P_SIZE)) for frame_idx in range(FRAMES)])
    obj_real = patches[:, 0][None]
    obj_imag = patches[:, 1][None]
    exit_real = probe_real * obj_real - probe_imag * obj_imag
    exit_imag = probe_real * obj_imag + probe_imag * obj_real
    wave_real, wave_imag = transform(exit_real, exit_imag, cosine_table, sine_table)
    power_sum = lax.optimization_barrier(jnp.sum(weights[:, None, None, None] * (wave_real * wave_real + wave_imag * wave_imag), axis=0))
    model_power = power_sum / total_weight
    factor = jnp.sqrt(measured_tile) / jnp.sqrt(model_power + intensity_offset) - 1.0
    diff_real, diff_imag = transform(wave_real * factor, wave_imag * factor, cosine_table, -sine_table)
    grad_real = lax.optimization_barrier(jnp.sum(probe_real * diff_real + probe_imag * diff_imag, axis=0))
    grad_imag = lax.optimization_barrier(jnp.sum(probe_real * diff_imag - probe_imag * diff_real, axis=0))
    gradient_sum = jnp.zeros((3, TILE, TILE), jnp.float32)
    for frame_idx in range(FRAMES):
        corner = (anchor, offsets[frame_idx, 0], offsets[frame_idx, 1])
        current = lax.dynamic_slice(gradient_sum, corner, (3, P_SIZE, P_SIZE))
        addition = jnp.stack([grad_real[frame_idx], grad_imag[frame_idx], illumination])
        gradient_sum = lax.dynamic_update_slice(gradient_sum, current + addition, corner)
    new_tile = tile_field + gradient_sum[:2] / (gradient_sum[2:3] + damping)
    probe_grad_real = lax.optimization_barrier(jnp.sum(obj_real * diff_real + obj_imag * diff_imag, axis=1))
    probe_grad_imag = lax.optimization_barrier(jnp.sum(obj_real * diff_imag - obj_imag * diff_real, axis=1))
    denominator = lax.optimization_barrier(jnp.sum(obj_real[0] * obj_real[0] + obj_imag[0] * obj_imag[0], axis=0))
    return (new_tile, jnp.stack([probe_grad_real, probe_grad_imag], axis=1), denominator)

def reference(object_field, probes, measured, positions, weights):
    cosine_table, sine_table = tables(P_SIZE)
    total_weight = jnp.sum(weights)
    probe_real = probes[:, 0][:, None]
    probe_imag = probes[:, 1][:, None]
    illumination = lax.optimization_barrier(jnp.sum(probes[:, 0] * probes[:, 0] + probes[:, 1] * probes[:, 1], axis=0))
    anchor = jnp.zeros((), jnp.int32)

    def per_tile(carry, tile_index):
        row_tile = tile_index // COLS_T
        col_tile = tile_index % COLS_T
        tile_field = lax.dynamic_slice(object_field, (anchor, row_tile * TILE, col_tile * TILE), (2, TILE, TILE))
        new_tile, probe_grad, denominator = tile_update(tile_field, probe_real, probe_imag, illumination, measured[row_tile, col_tile], positions[row_tile, col_tile], weights, total_weight, cosine_table, sine_table)
        return ((carry[0] + probe_grad, carry[1] + denominator), new_tile)
    start = (jnp.zeros((WAVES, 2, P_SIZE, P_SIZE), jnp.float32), jnp.zeros((P_SIZE, P_SIZE), jnp.float32))
    (probe_grad, denominator), new_tiles = lax.scan(per_tile, start, jnp.arange(ROWS_T * COLS_T, dtype=jnp.int32))
    new_tiles = new_tiles.reshape(ROWS_T, COLS_T, 2, TILE, TILE).transpose(2, 0, 3, 1, 4).reshape(2, NY, NX)
    new_probes = probes + probe_grad / (denominator + damping)
    return (new_tiles, new_probes)
```

```python
import functools
import math

import jax
import jax.numpy as jnp
import numpy as np
from jax import lax
from jax.experimental import pallas as pl
from jax.experimental.pallas import tpu as pltpu
from jax.sharding import PartitionSpec as P

damping = 1.0
intensity_offset = 0.1


def tables(length):
    indices = np.arange(length)
    angles = 2.0 * math.pi / length * (indices[:, None] * indices[None, :] % length)
    cosine = np.cos(angles) / math.sqrt(length)
    sine = -np.sin(angles) / math.sqrt(length)
    right = []
    for table in (cosine, sine - cosine, sine + cosine):
        high = table.astype(jnp.bfloat16)
        low = (table - high.astype(np.float64)).astype(jnp.bfloat16)
        right.append(np.concatenate([high, high, low], axis=0))
    right = np.stack(right)
    return right, np.ascontiguousarray(right.transpose(0, 2, 1))


def split(x):
    high = x.astype(jnp.bfloat16)
    low = (x - high.astype(jnp.float32)).astype(jnp.bfloat16)
    return high, low


def times_right(x, table):
    high, low = split(x)
    return jnp.dot(
        jnp.concatenate([high, low, high], axis=1), table, preferred_element_type=jnp.float32
    )


def times_left(x, table):
    high, low = split(x)
    return jnp.dot(
        table, jnp.concatenate([high, low, high], axis=0), preferred_element_type=jnp.float32
    )


def forward(real, imag, right, left):
    for times, table in ((times_right, right), (times_left, left)):
        both = times(real + imag, table[0])
        real, imag = both - times(imag, table[2]), both + times(real, table[1])
    return real, imag


def inverse(real, imag, right, left):
    for times, table in ((times_right, right), (times_left, left)):
        both = times(real + imag, table[0])
        real, imag = both + times(imag, table[1]), both - times(real, table[2])
    return real, imag


def step_kernel(
    pos, wts, obj, probes, meas, right, left, new_obj, q, e, patch, psi, hacc, light, grad, power
):
    waves = probes.shape[0]
    count = meas.shape[0]
    psize = probes.shape[-1]
    side = obj.shape[-1]
    tall = psize + 8
    total = wts[0]
    for w in range(1, waves):
        total = total + wts[w]
    inv_total = 1.0 / jnp.full((1, psize), total)
    light[...] = probes[0, 0] * probes[0, 0] + probes[0, 1] * probes[0, 1]

    def each_wave(start, body):
        if waves - start <= 2:
            for w in range(start, waves):
                body(w)
        else:
            pl.loop(start, waves)(body)

    def add_light(w):
        light[...] += probes[w, 0] * probes[w, 0] + probes[w, 1] * probes[w, 1]

    each_wave(1, add_light)
    new_obj[...] = jnp.zeros_like(new_obj)
    hacc[...] = jnp.zeros_like(hacc)
    q[...] = jnp.zeros_like(q)
    e[...] = jnp.zeros_like(e)

    @pl.loop(0, count)
    def _(f):
        r, c = pos[f, 0], pos[f, 1]
        back = lax.rem(side - c, side)
        base = pl.multiple_of(jnp.minimum(r // 8 * 8, side - tall), 8)
        shift = r - base
        for ch in range(2):
            rows = pltpu.roll(obj[ch, pl.ds(base, tall), :], back, 1)[:, :psize]
            patch[ch] = pltpu.roll(rows, lax.rem(tall - shift, tall), 0)[:psize]
        e[...] += patch[0] * patch[0] + patch[1] * patch[1]
        power[...] = jnp.zeros_like(power)

        def far(w):
            pr, pi = probes[w, 0], probes[w, 1]
            o_r, o_i = patch[0], patch[1]
            real, imag = forward(pr * o_r - pi * o_i, pr * o_i + pi * o_r, right, left)
            psi[w, 0] = real
            psi[w, 1] = imag
            power[...] += wts[w] * (real * real + imag * imag)

        each_wave(0, far)
        power[...] = (
            jnp.sqrt(meas[f]) / jnp.sqrt(power[...] * inv_total + intensity_offset) - 1.0
        )
        grad[...] = jnp.zeros_like(grad)

        def near(w):
            factor = power[...]
            real, imag = inverse(psi[w, 0] * factor, psi[w, 1] * factor, right, left)
            pr, pi = probes[w, 0], probes[w, 1]
            grad[0] += pr * real + pi * imag
            grad[1] += pr * imag - pi * real
            if isinstance(w, int) and w == 0:
                o_r, o_i = patch[0], patch[1]
                q[0] += o_r * real + o_i * imag
                q[1] += o_r * imag - o_i * real

        near(0)
        each_wave(1, near)

        def place(window):
            below = jnp.zeros((tall - psize, psize), jnp.float32)
            window = pltpu.roll(jnp.concatenate([window, below], 0), shift, 0)
            beside = jnp.zeros((tall, side - psize), jnp.float32)
            return pltpu.roll(jnp.concatenate([window, beside], 1), c, 1)

        for ch in range(2):
            new_obj[ch, pl.ds(base, tall), :] += place(grad[ch])
        hacc[pl.ds(base, tall), :] += place(light[...])

    scale = 1.0 / (hacc[...] + damping)
    for ch in range(2):
        new_obj[ch] = obj[ch] + new_obj[ch] * scale


def local(waves, object_field, probes, measured, positions, weights):
    psize = probes.shape[-1]
    side = object_field.shape[-1]
    right, left = tables(psize)
    all_probes, all_weights = [probes], [weights]
    for turn in range(1, waves):
        ring = [(i, (i + turn) % waves) for i in range(waves)]
        all_probes.append(lax.ppermute(probes, "wave", ring))
        all_weights.append(lax.ppermute(weights, "wave", ring))
    all_probes = jnp.concatenate(all_probes)
    all_weights = jnp.concatenate(all_weights)
    vmem = pl.BlockSpec(memory_space=pltpu.VMEM)
    smem = pl.BlockSpec(memory_space=pltpu.SMEM)
    f32 = jnp.float32
    new_object, q, e = pl.pallas_call(
        step_kernel,
        out_shape=(
            jax.ShapeDtypeStruct(object_field.shape, f32),
            jax.ShapeDtypeStruct((2, psize, psize), f32),
            jax.ShapeDtypeStruct((psize, psize), f32),
        ),
        in_specs=[smem, smem] + [vmem] * 5,
        out_specs=(vmem,) * 3,
        scratch_shapes=[
            pltpu.VMEM((2, psize, psize), f32),
            pltpu.VMEM((waves, 2, psize, psize), f32),
            pltpu.VMEM((side, side), f32),
            pltpu.VMEM((psize, psize), f32),
            pltpu.VMEM((2, psize, psize), f32),
            pltpu.VMEM((psize, psize), f32),
        ],
        compiler_params=pltpu.CompilerParams(vmem_limit_bytes=60 * 2**20),
    )(positions[0, 0], all_weights, object_field, all_probes, measured[0, 0], right, left)
    q, e = lax.psum((q, e), ("ty", "tx"))
    new_probes = probes + (q / (e + damping))[None]
    return (new_object, new_probes)


def solution(mesh):
    in_specs = (
        P(None, "ty", "tx"),
        P("wave", None, None, None),
        P("ty", "tx", None, None, None),
        P("ty", "tx", None, None),
        P("wave"),
    )
    out_specs = (P(None, "ty", "tx"), P("wave", None, None, None))
    body = functools.partial(local, mesh.shape["wave"])
    return jax.shard_map(body, mesh=mesh, in_specs=in_specs, out_specs=out_specs, check_vma=False)
```

```python
import functools
import math

import jax
import jax.numpy as jnp
import numpy as np
from jax import lax
from jax.experimental import pallas as pl
from jax.experimental.pallas import tpu as pltpu
from jax.sharding import PartitionSpec as P

damping = 1.0
intensity_offset = 0.1


def tables(length):
    indices = np.arange(length)
    angles = 2.0 * math.pi / length * (indices[:, None] * indices[None, :] % length)
    cosine = np.cos(angles) / math.sqrt(length)
    sine = -np.sin(angles) / math.sqrt(length)
    right = []
    for table in (cosine, sine - cosine, sine + cosine):
        high = table.astype(jnp.bfloat16)
        low = (table - high.astype(np.float64)).astype(jnp.bfloat16)
        right.append(np.concatenate([high, high, low], axis=0))
    right = np.stack(right)
    return right, np.ascontiguousarray(right.transpose(0, 2, 1))


def split(x):
    high = x.astype(jnp.bfloat16)
    low = (x - high.astype(jnp.float32)).astype(jnp.bfloat16)
    return high, low


def times_right(x, table):
    high, low = split(x)
    return jnp.dot(
        jnp.concatenate([high, low, high], axis=1), table, preferred_element_type=jnp.float32
    )


def times_left(x, table):
    high, low = split(x)
    return jnp.dot(
        table, jnp.concatenate([high, low, high], axis=0), preferred_element_type=jnp.float32
    )


def forward(real, imag, right, left):
    for times, table in ((times_right, right), (times_left, left)):
        both = times(real + imag, table[0])
        real, imag = both - times(imag, table[2]), both + times(real, table[1])
    return real, imag


def inverse(real, imag, right, left):
    for times, table in ((times_right, right), (times_left, left)):
        both = times(real + imag, table[0])
        real, imag = both + times(imag, table[1]), both - times(real, table[2])
    return real, imag


def step_kernel(
    pos, wts, obj, probes, meas, right, left, new_obj, q, e, patch, psi, hacc, light, grad, power
):
    waves = probes.shape[0]
    count = meas.shape[0]
    psize = probes.shape[-1]
    side = obj.shape[-1]
    tall = psize + 8
    total = wts[0]
    for w in range(1, waves):
        total = total + wts[w]
    inv_total = 1.0 / jnp.full((1, psize), total)
    light[...] = probes[0, 0] * probes[0, 0] + probes[0, 1] * probes[0, 1]

    def each_wave(start, body):
        if waves - start <= 2:
            for w in range(start, waves):
                body(w)
        else:
            pl.loop(start, waves)(body)

    def add_light(w):
        light[...] += probes[w, 0] * probes[w, 0] + probes[w, 1] * probes[w, 1]

    each_wave(1, add_light)
    new_obj[...] = jnp.zeros_like(new_obj)
    hacc[...] = jnp.zeros_like(hacc)
    q[...] = jnp.zeros_like(q)
    e[...] = jnp.zeros_like(e)

    @pl.loop(0, count)
    def _(f):
        r, c = pos[f, 0], pos[f, 1]
        back = lax.rem(side - c, side)
        base = pl.multiple_of(jnp.minimum(r // 8 * 8, side - tall), 8)
        shift = r - base
        for ch in range(2):
            rows = pltpu.roll(obj[ch, pl.ds(base, tall), :], back, 1)[:, :psize]
            patch[ch] = pltpu.roll(rows, lax.rem(tall - shift, tall), 0)[:psize]
        e[...] += patch[0] * patch[0] + patch[1] * patch[1]
        power[...] = jnp.zeros_like(power)

        def far(w):
            pr, pi = probes[w, 0], probes[w, 1]
            o_r, o_i = patch[0], patch[1]
            real, imag = forward(pr * o_r - pi * o_i, pr * o_i + pi * o_r, right, left)
            psi[w, 0] = real
            psi[w, 1] = imag
            power[...] += wts[w] * (real * real + imag * imag)

        each_wave(0, far)
        power[...] = (
            jnp.sqrt(meas[f]) / jnp.sqrt(power[...] * inv_total + intensity_offset) - 1.0
        )
        grad[...] = jnp.zeros_like(grad)

        def near(w):
            factor = power[...]
            real, imag = inverse(psi[w, 0] * factor, psi[w, 1] * factor, right, left)
            pr, pi = probes[w, 0], probes[w, 1]
            grad[0] += pr * real + pi * imag
            grad[1] += pr * imag - pi * real
            if isinstance(w, int) and w == 0:
                o_r, o_i = patch[0], patch[1]
                q[0] += o_r * real + o_i * imag
                q[1] += o_r * imag - o_i * real

        near(0)
        each_wave(1, near)

        def place(window):
            below = jnp.zeros((tall - psize, psize), jnp.float32)
            window = pltpu.roll(jnp.concatenate([window, below], 0), shift, 0)
            beside = jnp.zeros((tall, side - psize), jnp.float32)
            return pltpu.roll(jnp.concatenate([window, beside], 1), c, 1)

        for ch in range(2):
            new_obj[ch, pl.ds(base, tall), :] += place(grad[ch])
        hacc[pl.ds(base, tall), :] += place(light[...])

    scale = 1.0 / (hacc[...] + damping)
    for ch in range(2):
        new_obj[ch] = obj[ch] + new_obj[ch] * scale


def local(waves, object_field, probes, measured, positions, weights):
    psize = probes.shape[-1]
    side = object_field.shape[-1]
    right, left = tables(psize)
    all_probes, all_weights = [probes], [weights]
    for turn in range(1, waves):
        ring = [(i, (i + turn) % waves) for i in range(waves)]
        all_probes.append(lax.ppermute(probes, "wave", ring))
        all_weights.append(lax.ppermute(weights, "wave", ring))
    all_probes = jnp.concatenate(all_probes)
    all_weights = jnp.concatenate(all_weights)
    vmem = pl.BlockSpec(memory_space=pltpu.VMEM)
    smem = pl.BlockSpec(memory_space=pltpu.SMEM)
    f32 = jnp.float32
    new_object, q, e = pl.pallas_call(
        step_kernel,
        out_shape=(
            jax.ShapeDtypeStruct(object_field.shape, f32),
            jax.ShapeDtypeStruct((2, psize, psize), f32),
            jax.ShapeDtypeStruct((psize, psize), f32),
        ),
        in_specs=[smem, smem] + [vmem] * 5,
        out_specs=(vmem,) * 3,
        scratch_shapes=[
            pltpu.VMEM((2, psize, psize), f32),
            pltpu.VMEM((waves, 2, psize, psize), f32),
            pltpu.VMEM((side, side), f32),
            pltpu.VMEM((psize, psize), f32),
            pltpu.VMEM((2, psize, psize), f32),
            pltpu.VMEM((psize, psize), f32),
        ],
        compiler_params=pltpu.CompilerParams(vmem_limit_bytes=60 * 2**20),
    )(positions[0, 0], all_weights, object_field, all_probes, measured[0, 0], right, left)
    q, e = lax.psum((q, e), ("ty", "tx"))
    new_probes = probes + (q / (e + damping))[None]
    return (new_object, new_probes)


def at(pos, f, side, tall):
    r, c = pos[f, 0], pos[f, 1]
    base = pl.multiple_of(jnp.minimum(r // 8 * 8, side - tall), 8)
    return base, r - base, c


def window_kernel(pos, obj, patch, e):
    psize, side = patch.shape[-1], obj.shape[-1]
    tall = psize + 8
    f = pl.program_id(0)
    base, shift, c = at(pos, f, side, tall)
    power = jnp.zeros((psize, psize), jnp.float32)
    for ch in range(2):
        rows = pltpu.roll(obj[ch, pl.ds(base, tall), :], lax.rem(side - c, side), 1)[:, :psize]
        rows = pltpu.roll(rows, lax.rem(tall - shift, tall), 0)[:psize]
        patch[0, ch] = rows
        power += rows * rows

    @pl.when(f == 0)
    def _():
        e[0] = power

    @pl.when(f > 0)
    def _():
        e[0] += power


def scatter_kernel(pos, obj, grad, light, new_obj, hacc):
    psize, side = grad.shape[-1], obj.shape[-1]
    tall = psize + 8
    f = pl.program_id(0)
    base, shift, c = at(pos, f, side, tall)

    @pl.when(f == 0)
    def _():
        new_obj[...] = jnp.zeros_like(new_obj)
        hacc[...] = jnp.zeros_like(hacc)

    def place(window):
        below = jnp.zeros((tall - psize, psize), jnp.float32)
        window = pltpu.roll(jnp.concatenate([window, below], 0), shift, 0)
        beside = jnp.zeros((tall, side - psize), jnp.float32)
        return pltpu.roll(jnp.concatenate([window, beside], 1), c, 1)

    for ch in range(2):
        new_obj[ch, pl.ds(base, tall), :] += place(grad[0, ch])
    hacc[pl.ds(base, tall), :] += place(light[...])

    @pl.when(f == pl.num_programs(0) - 1)
    def _():
        scale = 1.0 / (hacc[...] + damping)
        for ch in range(2):
            new_obj[ch] = obj[ch] + new_obj[ch] * scale


def pair_kernel(
    bits, rows_of_tiles,
    wts, patch, e, probes, meas, right, left,
    grad, light, new_probes,
    other, wmine, wother, psi, q, q_sums, q_got, e_sums, e_got, q_pieces, e_pieces, result,
    send, recv,
):
    count = meas.shape[0]
    psize = probes.shape[-1]
    f32 = jnp.float32
    wave, ty, tx = lax.axis_index("wave"), lax.axis_index("ty"), lax.axis_index("tx")
    mate = {"wave": 1 - wave}
    halves = []
    for bit in range(bits):
        mine = tx // 2**bit % 2
        halves.append((mine, {"tx": tx + (1 - 2 * mine) * 2**bit}))
    others = [{"ty": lax.rem(ty + d, rows_of_tiles)} for d in range(1, rows_of_tiles)]

    barrier = pltpu.get_barrier_semaphore()
    partners = [mate] + [h[1] for h in halves] + others
    for partner in partners:
        pl.semaphore_signal(
            barrier, inc=1, device_id=partner, device_id_type=pl.DeviceIdType.MESH
        )
    pl.semaphore_wait(barrier, len(partners))

    used = [0]

    def ship(src, dst, partner):
        k = used[0]
        used[0] += 1
        copy = pltpu.make_async_remote_copy(
            src_ref=src, dst_ref=dst, send_sem=send.at[k], recv_sem=recv.at[k],
            device_id=partner, device_id_type=pl.DeviceIdType.MESH,
        )
        copy.start()
        return copy

    wmine[...] = jnp.full(wmine.shape, wts[0], f32)
    probe_copies = [ship(probes, other, mate), ship(wmine, wother, mate)]

    def reduce_rows(source, sums, got, pieces):
        rows = psize
        for step, (mine, partner) in enumerate(halves):
            rows //= 2
            away = pl.ds(pl.multiple_of((1 - mine) * rows, 8), rows)
            copy = ship(source.at[:, away], got[step], partner)
            yield
            copy.wait()
            keep = pl.ds(pl.multiple_of(mine * rows, 8), rows)
            sums[step][...] = source[:, keep] + got[step][...]
            source = sums[step]
        rows //= rows_of_tiles
        copies = []
        for d, partner in enumerate(others):
            away = pl.ds(pl.multiple_of(partner["ty"] * rows, 8), rows)
            copies.append(ship(source.at[:, away], pieces.at[d], partner))
        yield
        for copy in copies:
            copy.wait()
        whole = source[:, pl.ds(pl.multiple_of(ty * rows, 8), rows)]
        for d in range(len(others)):
            whole = whole + pieces[d]
        pieces[len(others)] = whole
        yield

    def spread_rows():
        rows = psize // 2**bits // rows_of_tiles
        first = 0
        height = psize
        for mine, _ in halves:
            height //= 2
            first = first + mine * height
        here = pl.ds(pl.multiple_of(first + ty * rows, 8), rows)
        whole = q_pieces[len(others)] / (e_pieces[len(others)] + damping)
        result[:, here] = probes[0, :, here] + whole
        copies = [ship(result.at[:, here], result.at[:, here], p) for p in others]
        yield
        for copy in copies:
            copy.wait()
        for mine, partner in reversed(halves):
            here = pl.ds(pl.multiple_of(first, 8), height)
            copy = ship(result.at[:, here], result.at[:, here], partner)
            yield
            copy.wait()
            first = first - mine * height
            height *= 2
        yield

    def near(f, side_probes, w):
        pr, pi = side_probes[0, 0], side_probes[0, 1]
        o_r, o_i = patch[f, 0], patch[f, 1]
        real, imag = forward(pr * o_r - pi * o_i, pr * o_i + pi * o_r, right, left)
        psi[w, f, 0] = real
        psi[w, f, 1] = imag

    def loop(low, high, body):
        if high > low:
            pl.loop(low, high)(body)

    lighting = reduce_rows(e, e_sums, e_got, e_pieces)
    marks = [count * i // (bits + 1) for i in range(bits + 2)]
    for low, high in zip(marks, marks[1:]):
        next(lighting)
        loop(low, high, lambda f: near(f, probes, 0))
    next(lighting)
    for copy in probe_copies:
        copy.wait()

    w_0, w_1 = wmine[0:1, 0:1], wother[0:1, 0:1]
    total = w_0 + w_1
    w_0, w_1 = w_0 / total, w_1 / total
    light[...] = (
        probes[0, 0] * probes[0, 0] + probes[0, 1] * probes[0, 1]
        + other[0, 0] * other[0, 0] + other[0, 1] * other[0, 1]
    )

    def both(f):
        near(f, other, 1)
        power = w_0 * (psi[0, f, 0] * psi[0, f, 0] + psi[0, f, 1] * psi[0, f, 1])
        power += w_1 * (psi[1, f, 0] * psi[1, f, 0] + psi[1, f, 1] * psi[1, f, 1])
        factor = jnp.sqrt(meas[f]) / jnp.sqrt(power + intensity_offset) - 1.0
        for w in range(2):
            for ch in range(2):
                psi[w, f, ch] *= factor

    loop(0, count, both)
    q[...] = jnp.zeros_like(q)

    def own(f):
        real, imag = inverse(psi[0, f, 0], psi[0, f, 1], right, left)
        pr, pi = probes[0, 0], probes[0, 1]
        o_r, o_i = patch[f, 0], patch[f, 1]
        grad[f, 0] = pr * real + pi * imag
        grad[f, 1] = pr * imag - pi * real
        q[0] += o_r * real + o_i * imag
        q[1] += o_r * imag - o_i * real

    loop(0, count, own)

    def rest(f):
        real, imag = inverse(psi[1, f, 0], psi[1, f, 1], right, left)
        pr, pi = other[0, 0], other[0, 1]
        grad[f, 0] += pr * real + pi * imag
        grad[f, 1] += pr * imag - pi * real

    gather = reduce_rows(q, q_sums, q_got, q_pieces)
    phases = 2 * (bits + 1)
    done = 0

    def work(phase):
        nonlocal done
        later = 1 + (count - 1) * phase // (phases - 2) if phase else 1
        loop(done, min(later, count), rest)
        done = min(later, count)

    for phase in range(bits + 1):
        next(gather)
        work(phase)
    next(gather)
    out = spread_rows()
    next(out)
    for phase in range(bits + 1, phases):
        work(phase)
        next(out)
    new_probes[0] = result[...]


def pair_step(bits, rows_of_tiles, object_field, probes, measured, positions, weights):
    psize = probes.shape[-1]
    side = object_field.shape[-1]
    count = measured.shape[2]
    right, left = tables(psize)
    f32 = jnp.float32
    steps = bits + rows_of_tiles - 1
    copies = 2 + 3 * steps

    def buffers(planes):
        heights = [psize // 2 ** (b + 1) for b in range(bits)]
        halves = [pltpu.VMEM((planes, h, psize), f32) for h in heights]
        return halves

    def pieces(planes):
        rows = psize // 2**bits // rows_of_tiles
        return pltpu.VMEM((rows_of_tiles, planes, rows, psize), f32)

    vmem = pl.BlockSpec(memory_space=pltpu.VMEM)
    smem = pl.BlockSpec(memory_space=pltpu.SMEM)
    one_frame = pl.BlockSpec((1, 2, psize, psize), lambda f: (f, 0, 0, 0))
    frames = jax.ShapeDtypeStruct((count, 2, psize, psize), f32)
    image = jax.ShapeDtypeStruct((1, psize, psize), f32)
    room = pltpu.CompilerParams(vmem_limit_bytes=20 * 2**20)
    patches, e = pl.pallas_call(
        window_kernel,
        grid=(count,),
        out_shape=(frames, image),
        in_specs=[smem, vmem],
        out_specs=(one_frame, vmem),
        compiler_params=room,
    )(positions[0, 0], object_field)
    grad, light, new_probes = pl.pallas_call(
        functools.partial(pair_kernel, bits, rows_of_tiles),
        out_shape=(
            frames,
            jax.ShapeDtypeStruct((psize, psize), f32),
            jax.ShapeDtypeStruct(probes.shape, f32),
        ),
        in_specs=[smem] + [vmem] * 6,
        out_specs=(vmem,) * 3,
        scratch_shapes=[
            pltpu.VMEM(probes.shape, f32),
            pltpu.VMEM((8, 128), f32),
            pltpu.VMEM((8, 128), f32),
            pltpu.VMEM((2, count, 2, psize, psize), f32),
            pltpu.VMEM((2, psize, psize), f32),
            buffers(2),
            buffers(2),
            buffers(1),
            buffers(1),
            pieces(2),
            pieces(1),
            pltpu.VMEM((2, psize, psize), f32),
            pltpu.SemaphoreType.DMA((copies,)),
            pltpu.SemaphoreType.DMA((copies,)),
        ],
        compiler_params=pltpu.CompilerParams(
            vmem_limit_bytes=40 * 2**20, collective_id=0, has_side_effects=True
        ),
    )(weights, patches, e, probes, measured[0, 0], right, left)
    new_object = pl.pallas_call(
        scatter_kernel,
        grid=(count,),
        out_shape=jax.ShapeDtypeStruct(object_field.shape, f32),
        in_specs=[smem, vmem, one_frame, vmem],
        out_specs=vmem,
        scratch_shapes=[pltpu.VMEM((side, side), f32)],
        compiler_params=room,
    )(positions[0, 0], object_field, grad, light)
    return (new_object, new_probes)


def solution(mesh):
    in_specs = (
        P(None, "ty", "tx"),
        P("wave", None, None, None),
        P("ty", "tx", None, None, None),
        P("ty", "tx", None, None),
        P("wave"),
    )
    out_specs = (P(None, "ty", "tx"), P("wave", None, None, None))
    waves, rows_of_tiles, tiles = (mesh.shape[axis] for axis in ("wave", "ty", "tx"))
    bits = tiles.bit_length() - 1
    if waves == 2 and rows_of_tiles > 1 and bits >= 1 and 2**bits == tiles:
        body = functools.partial(pair_step, bits, rows_of_tiles)
    else:
        body = functools.partial(local, waves)
    return jax.shard_map(body, mesh=mesh, in_specs=in_specs, out_specs=out_specs, check_vma=False)
```

```python
import functools
import math

import jax
import jax.numpy as jnp
import numpy as np
from jax import lax
from jax.experimental import pallas as pl
from jax.experimental.pallas import tpu as pltpu
from jax.sharding import PartitionSpec as P

damping = 1.0
intensity_offset = 0.1


def tables(length):
    indices = np.arange(length)
    angles = 2.0 * math.pi / length * (indices[:, None] * indices[None, :] % length)
    cosine = np.cos(angles) / math.sqrt(length)
    sine = -np.sin(angles) / math.sqrt(length)
    half = length // 2
    parts = []
    for odd in range(2):
        c, s = cosine[:half, odd::2], sine[:half, odd::2]
        parts.append(np.block([[c, s], [-s, c]]))
    both = []
    for table in parts + [part.T for part in parts]:
        high = table.astype(jnp.bfloat16)
        low = (table - high.astype(np.float64)).astype(jnp.bfloat16)
        both.append(np.stack([high, low]))
    order = np.concatenate([indices[0::2], indices[1::2]])
    shuffle = (indices[:, None] == order[None, :]).astype(jnp.bfloat16)
    return np.stack(both), np.stack([shuffle, shuffle.T])


def split(x):
    high = x.astype(jnp.bfloat16)
    low = (x - high.astype(jnp.float32)).astype(jnp.bfloat16)
    return high, low


def times(x, table, which, axis):
    high, low = split(x)
    x = jnp.concatenate([high, low, high], axis=axis)
    which = which if axis == 1 else (which + 2) % 4
    high, low = table[which, 0], table[which, 1]
    table = jnp.concatenate([high, high, low], axis=1 - axis)
    pair = (x, table) if axis == 1 else (table, x)
    return jnp.dot(*pair, preferred_element_type=jnp.float32)


def halves_of(x, axis):
    half = x.shape[axis] // 2
    return (x[:, :half], x[:, half:]) if axis == 1 else (x[:half], x[half:])


def forward(real, imag, table):
    for axis in (1, 0):
        (r0, r1), (i0, i1) = halves_of(real, axis), halves_of(imag, axis)
        even = times(jnp.concatenate([r0 + r1, i0 + i1], axis), table, 0, axis)
        odd = times(jnp.concatenate([r0 - r1, i0 - i1], axis), table, 1, axis)
        (er, ei), (o_r, oi) = halves_of(even, axis), halves_of(odd, axis)
        real = jnp.concatenate([er, o_r], axis)
        imag = jnp.concatenate([ei, oi], axis)
    return real, imag


def inverse(real, imag, table):
    for axis in (1, 0):
        (er, o_r), (ei, oi) = halves_of(real, axis), halves_of(imag, axis)
        even = times(jnp.concatenate([er, ei], axis), table, 2, axis)
        odd = times(jnp.concatenate([o_r, oi], axis), table, 3, axis)
        (r0, i0), (r1, i1) = halves_of(even + odd, axis), halves_of(even - odd, axis)
        real = jnp.concatenate([r0, r1], axis)
        imag = jnp.concatenate([i0, i1], axis)
    return real, imag


def amplitude(meas, f, order):
    root = jnp.sqrt(meas[f])
    for axis in (1, 0):
        both = jnp.concatenate(split(root), axis)
        twice = jnp.concatenate([order[1 - axis]] * 2, 1 - axis)
        pair = (both, twice) if axis == 1 else (twice, both)
        root = jnp.dot(*pair, preferred_element_type=jnp.float32)
    return root


def step_kernel(
    pos, wts, obj, probes, meas, table, order, new_obj, q, e, patch, psi, hacc, light, grad, power
):
    waves = probes.shape[0]
    count = meas.shape[0]
    psize = probes.shape[-1]
    side = obj.shape[-1]
    tall = psize + 8
    total = wts[0]
    for w in range(1, waves):
        total = total + wts[w]
    inv_total = 1.0 / jnp.full((1, psize), total)
    light[...] = probes[0, 0] * probes[0, 0] + probes[0, 1] * probes[0, 1]

    def each_wave(start, body):
        if waves - start <= 2:
            for w in range(start, waves):
                body(w)
        else:
            pl.loop(start, waves)(body)

    def add_light(w):
        light[...] += probes[w, 0] * probes[w, 0] + probes[w, 1] * probes[w, 1]

    each_wave(1, add_light)
    new_obj[...] = jnp.zeros_like(new_obj)
    hacc[...] = jnp.zeros_like(hacc)
    q[...] = jnp.zeros_like(q)
    e[...] = jnp.zeros_like(e)

    @pl.loop(0, count)
    def _(f):
        r, c = pos[f, 0], pos[f, 1]
        back = lax.rem(side - c, side)
        base = pl.multiple_of(jnp.minimum(r // 8 * 8, side - tall), 8)
        shift = r - base
        for ch in range(2):
            rows = pltpu.roll(obj[ch, pl.ds(base, tall), :], back, 1)[:, :psize]
            patch[ch] = pltpu.roll(rows, lax.rem(tall - shift, tall), 0)[:psize]
        e[...] += patch[0] * patch[0] + patch[1] * patch[1]
        power[...] = jnp.zeros_like(power)

        def far(w):
            pr, pi = probes[w, 0], probes[w, 1]
            o_r, o_i = patch[0], patch[1]
            real, imag = forward(pr * o_r - pi * o_i, pr * o_i + pi * o_r, table)
            psi[w, 0] = real
            psi[w, 1] = imag
            power[...] += wts[w] * (real * real + imag * imag)

        each_wave(0, far)
        power[...] = (
            amplitude(meas, f, order) / jnp.sqrt(power[...] * inv_total + intensity_offset)
            - 1.0
        )
        grad[...] = jnp.zeros_like(grad)

        def near(w):
            factor = power[...]
            real, imag = inverse(psi[w, 0] * factor, psi[w, 1] * factor, table)
            pr, pi = probes[w, 0], probes[w, 1]
            grad[0] += pr * real + pi * imag
            grad[1] += pr * imag - pi * real
            if isinstance(w, int) and w == 0:
                o_r, o_i = patch[0], patch[1]
                q[0] += o_r * real + o_i * imag
                q[1] += o_r * imag - o_i * real

        near(0)
        each_wave(1, near)

        def place(window):
            below = jnp.zeros((tall - psize, psize), jnp.float32)
            window = pltpu.roll(jnp.concatenate([window, below], 0), shift, 0)
            beside = jnp.zeros((tall, side - psize), jnp.float32)
            return pltpu.roll(jnp.concatenate([window, beside], 1), c, 1)

        for ch in range(2):
            new_obj[ch, pl.ds(base, tall), :] += place(grad[ch])
        hacc[pl.ds(base, tall), :] += place(light[...])

    scale = 1.0 / (hacc[...] + damping)
    for ch in range(2):
        new_obj[ch] = obj[ch] + new_obj[ch] * scale


def local(waves, object_field, probes, measured, positions, weights):
    psize = probes.shape[-1]
    side = object_field.shape[-1]
    table, order = tables(psize)
    all_probes, all_weights = [probes], [weights]
    for turn in range(1, waves):
        ring = [(i, (i + turn) % waves) for i in range(waves)]
        all_probes.append(lax.ppermute(probes, "wave", ring))
        all_weights.append(lax.ppermute(weights, "wave", ring))
    all_probes = jnp.concatenate(all_probes)
    all_weights = jnp.concatenate(all_weights)
    vmem = pl.BlockSpec(memory_space=pltpu.VMEM)
    smem = pl.BlockSpec(memory_space=pltpu.SMEM)
    f32 = jnp.float32
    new_object, q, e = pl.pallas_call(
        step_kernel,
        out_shape=(
            jax.ShapeDtypeStruct(object_field.shape, f32),
            jax.ShapeDtypeStruct((2, psize, psize), f32),
            jax.ShapeDtypeStruct((psize, psize), f32),
        ),
        in_specs=[smem, smem] + [vmem] * 5,
        out_specs=(vmem,) * 3,
        scratch_shapes=[
            pltpu.VMEM((2, psize, psize), f32),
            pltpu.VMEM((waves, 2, psize, psize), f32),
            pltpu.VMEM((side, side), f32),
            pltpu.VMEM((psize, psize), f32),
            pltpu.VMEM((2, psize, psize), f32),
            pltpu.VMEM((psize, psize), f32),
        ],
        compiler_params=pltpu.CompilerParams(vmem_limit_bytes=60 * 2**20),
    )(positions[0, 0], all_weights, object_field, all_probes, measured[0, 0], table, order)
    q, e = lax.psum((q, e), ("ty", "tx"))
    new_probes = probes + (q / (e + damping))[None]
    return (new_object, new_probes)


def at(pos, f, side, tall):
    r, c = pos[f, 0], pos[f, 1]
    base = pl.multiple_of(jnp.minimum(r // 8 * 8, side - tall), 8)
    return base, r - base, c


def window_kernel(pos, obj, patch, e):
    psize, side = patch.shape[-1], obj.shape[-1]
    tall = psize + 8
    f = pl.program_id(0)
    base, shift, c = at(pos, f, side, tall)
    power = jnp.zeros((psize, psize), jnp.float32)
    for ch in range(2):
        rows = pltpu.roll(obj[ch, pl.ds(base, tall), :], lax.rem(side - c, side), 1)[:, :psize]
        rows = pltpu.roll(rows, lax.rem(tall - shift, tall), 0)[:psize]
        patch[0, ch] = rows
        power += rows * rows

    @pl.when(f == 0)
    def _():
        e[0] = power

    @pl.when(f > 0)
    def _():
        e[0] += power


def scatter_kernel(pos, obj, grad, light, new_obj, hacc):
    psize, side = grad.shape[-1], obj.shape[-1]
    tall = psize + 8
    f = pl.program_id(0)
    base, shift, c = at(pos, f, side, tall)

    @pl.when(f == 0)
    def _():
        new_obj[...] = jnp.zeros_like(new_obj)
        hacc[...] = jnp.zeros_like(hacc)

    def place(window):
        below = jnp.zeros((tall - psize, psize), jnp.float32)
        window = pltpu.roll(jnp.concatenate([window, below], 0), shift, 0)
        beside = jnp.zeros((tall, side - psize), jnp.float32)
        return pltpu.roll(jnp.concatenate([window, beside], 1), c, 1)

    for ch in range(2):
        new_obj[ch, pl.ds(base, tall), :] += place(grad[0, ch])
    hacc[pl.ds(base, tall), :] += place(light[...])

    @pl.when(f == pl.num_programs(0) - 1)
    def _():
        scale = 1.0 / (hacc[...] + damping)
        for ch in range(2):
            new_obj[ch] = obj[ch] + new_obj[ch] * scale


def pair_kernel(
    bits, rows_of_tiles,
    wts, patch, e, probes, meas, table, order,
    grad, light, new_probes,
    other, wmine, wother, psi, q, q_sums, q_got, e_sums, e_got, q_pieces, e_pieces, result,
    send, recv,
):
    count = meas.shape[0]
    psize = probes.shape[-1]
    f32 = jnp.float32
    wave, ty, tx = lax.axis_index("wave"), lax.axis_index("ty"), lax.axis_index("tx")
    mate = {"wave": 1 - wave}
    halves = []
    for bit in range(bits):
        mine = tx // 2**bit % 2
        halves.append((mine, {"tx": tx + (1 - 2 * mine) * 2**bit}))
    others = [{"ty": lax.rem(ty + d, rows_of_tiles)} for d in range(1, rows_of_tiles)]

    barrier = pltpu.get_barrier_semaphore()
    partners = [mate] + [h[1] for h in halves] + others
    for partner in partners:
        pl.semaphore_signal(
            barrier, inc=1, device_id=partner, device_id_type=pl.DeviceIdType.MESH
        )
    pl.semaphore_wait(barrier, len(partners))

    used = [0]

    def ship(src, dst, partner):
        k = used[0]
        used[0] += 1
        copy = pltpu.make_async_remote_copy(
            src_ref=src, dst_ref=dst, send_sem=send.at[k], recv_sem=recv.at[k],
            device_id=partner, device_id_type=pl.DeviceIdType.MESH,
        )
        copy.start()
        return copy

    wmine[...] = jnp.full(wmine.shape, wts[0], f32)
    probe_copies = [ship(probes, other, mate), ship(wmine, wother, mate)]

    def reduce_rows(source, sums, got, pieces):
        rows = psize
        for step, (mine, partner) in enumerate(halves):
            rows //= 2
            away = pl.ds(pl.multiple_of((1 - mine) * rows, 8), rows)
            copy = ship(source.at[:, away], got[step], partner)
            yield
            copy.wait()
            keep = pl.ds(pl.multiple_of(mine * rows, 8), rows)
            sums[step][...] = source[:, keep] + got[step][...]
            source = sums[step]
        rows //= rows_of_tiles
        copies = []
        for d, partner in enumerate(others):
            away = pl.ds(pl.multiple_of(partner["ty"] * rows, 8), rows)
            copies.append(ship(source.at[:, away], pieces.at[d], partner))
        yield
        for copy in copies:
            copy.wait()
        whole = source[:, pl.ds(pl.multiple_of(ty * rows, 8), rows)]
        for d in range(len(others)):
            whole = whole + pieces[d]
        pieces[len(others)] = whole
        yield

    def spread_rows():
        rows = psize // 2**bits // rows_of_tiles
        first = 0
        height = psize
        for mine, _ in halves:
            height //= 2
            first = first + mine * height
        here = pl.ds(pl.multiple_of(first + ty * rows, 8), rows)
        whole = q_pieces[len(others)] / (e_pieces[len(others)] + damping)
        result[:, here] = probes[0, :, here] + whole
        copies = [ship(result.at[:, here], result.at[:, here], p) for p in others]
        yield
        for copy in copies:
            copy.wait()
        for mine, partner in reversed(halves):
            here = pl.ds(pl.multiple_of(first, 8), height)
            copy = ship(result.at[:, here], result.at[:, here], partner)
            yield
            copy.wait()
            first = first - mine * height
            height *= 2
        yield

    def near(f, side_probes, w):
        pr, pi = side_probes[0, 0], side_probes[0, 1]
        o_r, o_i = patch[f, 0], patch[f, 1]
        real, imag = forward(pr * o_r - pi * o_i, pr * o_i + pi * o_r, table)
        psi[w, f, 0] = real
        psi[w, f, 1] = imag

    def loop(low, high, body):
        if high > low:
            pl.loop(low, high)(body)

    lighting = reduce_rows(e, e_sums, e_got, e_pieces)
    marks = [count * i // (bits + 1) for i in range(bits + 2)]
    for low, high in zip(marks, marks[1:]):
        next(lighting)
        loop(low, high, lambda f: near(f, probes, 0))
    next(lighting)
    for copy in probe_copies:
        copy.wait()

    w_0, w_1 = wmine[0:1, 0:1], wother[0:1, 0:1]
    total = w_0 + w_1
    w_0, w_1 = w_0 / total, w_1 / total
    light[...] = (
        probes[0, 0] * probes[0, 0] + probes[0, 1] * probes[0, 1]
        + other[0, 0] * other[0, 0] + other[0, 1] * other[0, 1]
    )

    def both(f):
        near(f, other, 1)
        power = w_0 * (psi[0, f, 0] * psi[0, f, 0] + psi[0, f, 1] * psi[0, f, 1])
        power += w_1 * (psi[1, f, 0] * psi[1, f, 0] + psi[1, f, 1] * psi[1, f, 1])
        factor = amplitude(meas, f, order) / jnp.sqrt(power + intensity_offset) - 1.0
        for w in range(2):
            for ch in range(2):
                psi[w, f, ch] *= factor

    loop(0, count, both)
    q[...] = jnp.zeros_like(q)

    def own(f):
        real, imag = inverse(psi[0, f, 0], psi[0, f, 1], table)
        pr, pi = probes[0, 0], probes[0, 1]
        o_r, o_i = patch[f, 0], patch[f, 1]
        grad[f, 0] = pr * real + pi * imag
        grad[f, 1] = pr * imag - pi * real
        q[0] += o_r * real + o_i * imag
        q[1] += o_r * imag - o_i * real

    loop(0, count, own)

    def rest(f):
        real, imag = inverse(psi[1, f, 0], psi[1, f, 1], table)
        pr, pi = other[0, 0], other[0, 1]
        grad[f, 0] += pr * real + pi * imag
        grad[f, 1] += pr * imag - pi * real

    gather = reduce_rows(q, q_sums, q_got, q_pieces)
    phases = 2 * (bits + 1)
    done = 0

    def work(phase):
        nonlocal done
        later = 1 + (count - 1) * phase // (phases - 2) if phase else 1
        loop(done, min(later, count), rest)
        done = min(later, count)

    for phase in range(bits + 1):
        next(gather)
        work(phase)
    next(gather)
    out = spread_rows()
    next(out)
    for phase in range(bits + 1, phases):
        work(phase)
        next(out)
    new_probes[0] = result[...]


def pair_step(bits, rows_of_tiles, object_field, probes, measured, positions, weights):
    psize = probes.shape[-1]
    side = object_field.shape[-1]
    count = measured.shape[2]
    table, order = tables(psize)
    f32 = jnp.float32
    steps = bits + rows_of_tiles - 1
    copies = 2 + 3 * steps

    def buffers(planes):
        heights = [psize // 2 ** (b + 1) for b in range(bits)]
        halves = [pltpu.VMEM((planes, h, psize), f32) for h in heights]
        return halves

    def pieces(planes):
        rows = psize // 2**bits // rows_of_tiles
        return pltpu.VMEM((rows_of_tiles, planes, rows, psize), f32)

    vmem = pl.BlockSpec(memory_space=pltpu.VMEM)
    smem = pl.BlockSpec(memory_space=pltpu.SMEM)
    one_frame = pl.BlockSpec((1, 2, psize, psize), lambda f: (f, 0, 0, 0))
    frames = jax.ShapeDtypeStruct((count, 2, psize, psize), f32)
    image = jax.ShapeDtypeStruct((1, psize, psize), f32)
    room = pltpu.CompilerParams(vmem_limit_bytes=60 * 2**20)
    patches, e = pl.pallas_call(
        window_kernel,
        grid=(count,),
        out_shape=(frames, image),
        in_specs=[smem, vmem],
        out_specs=(one_frame, vmem),
        compiler_params=room,
    )(positions[0, 0], object_field)
    grad, light, new_probes = pl.pallas_call(
        functools.partial(pair_kernel, bits, rows_of_tiles),
        out_shape=(
            frames,
            jax.ShapeDtypeStruct((psize, psize), f32),
            jax.ShapeDtypeStruct(probes.shape, f32),
        ),
        in_specs=[smem] + [vmem] * 6,
        out_specs=(vmem,) * 3,
        scratch_shapes=[
            pltpu.VMEM(probes.shape, f32),
            pltpu.VMEM((8, 128), f32),
            pltpu.VMEM((8, 128), f32),
            pltpu.VMEM((2, count, 2, psize, psize), f32),
            pltpu.VMEM((2, psize, psize), f32),
            buffers(2),
            buffers(2),
            buffers(1),
            buffers(1),
            pieces(2),
            pieces(1),
            pltpu.VMEM((2, psize, psize), f32),
            pltpu.SemaphoreType.DMA((copies,)),
            pltpu.SemaphoreType.DMA((copies,)),
        ],
        compiler_params=pltpu.CompilerParams(
            vmem_limit_bytes=60 * 2**20, collective_id=0, has_side_effects=True
        ),
    )(weights, patches, e, probes, measured[0, 0], table, order)
    new_object = pl.pallas_call(
        scatter_kernel,
        grid=(count,),
        out_shape=jax.ShapeDtypeStruct(object_field.shape, f32),
        in_specs=[smem, vmem, one_frame, vmem],
        out_specs=vmem,
        scratch_shapes=[pltpu.VMEM((side, side), f32)],
        compiler_params=room,
    )(positions[0, 0], object_field, grad, light)
    return (new_object, new_probes)


def solution(mesh):
    in_specs = (
        P(None, "ty", "tx"),
        P("wave", None, None, None),
        P("ty", "tx", None, None, None),
        P("ty", "tx", None, None),
        P("wave"),
    )
    out_specs = (P(None, "ty", "tx"), P("wave", None, None, None))
    waves, rows_of_tiles, tiles = (mesh.shape[axis] for axis in ("wave", "ty", "tx"))
    bits = tiles.bit_length() - 1
    if waves == 2 and rows_of_tiles > 1 and bits >= 1 and 2**bits == tiles:
        body = functools.partial(pair_step, bits, rows_of_tiles)
    else:
        body = functools.partial(local, waves)
    return jax.shard_map(body, mesh=mesh, in_specs=in_specs, out_specs=out_specs, check_vma=False)
```

```python
import functools
import math

import jax
import jax.numpy as jnp
import numpy as np
from jax import lax
from jax.experimental import pallas as pl
from jax.experimental.pallas import tpu as pltpu
from jax.sharding import PartitionSpec as P

damping = 1.0
intensity_offset = 0.1


def tables(length):
    indices = np.arange(length)
    angles = 2.0 * math.pi / length * (indices[:, None] * indices[None, :] % length)
    cosine = np.cos(angles) / math.sqrt(length)
    sine = -np.sin(angles) / math.sqrt(length)
    half = length // 2
    parts = []
    for odd in range(2):
        c, s = cosine[:half, odd::2], sine[:half, odd::2]
        parts.append(np.block([[c, s], [-s, c]]))
    both = []
    for table in parts + [part.T for part in parts]:
        high = table.astype(jnp.bfloat16)
        low = (table - high.astype(np.float64)).astype(jnp.bfloat16)
        both.append(np.stack([high, low]))
    order = np.concatenate([indices[0::2], indices[1::2]])
    shuffle = (indices[:, None] == order[None, :]).astype(jnp.bfloat16)
    return np.stack(both), np.stack([shuffle, shuffle.T])


def split(x):
    high = x.astype(jnp.bfloat16)
    low = (x - high.astype(jnp.float32)).astype(jnp.bfloat16)
    return high, low


def times(x, table, which, axis):
    high, low = split(x)
    x = jnp.concatenate([high, low, high], axis=axis)
    which = which if axis == 1 else (which + 2) % 4
    high, low = table[which, 0], table[which, 1]
    table = jnp.concatenate([high, high, low], axis=1 - axis)
    pair = (x, table) if axis == 1 else (table, x)
    return jnp.dot(*pair, preferred_element_type=jnp.float32)


def halves_of(x, axis):
    half = x.shape[axis] // 2
    return (x[:, :half], x[:, half:]) if axis == 1 else (x[:half], x[half:])


def forward(real, imag, table):
    for axis in (1, 0):
        (r0, r1), (i0, i1) = halves_of(real, axis), halves_of(imag, axis)
        even = times(jnp.concatenate([r0 + r1, i0 + i1], axis), table, 0, axis)
        odd = times(jnp.concatenate([r0 - r1, i0 - i1], axis), table, 1, axis)
        (er, ei), (o_r, oi) = halves_of(even, axis), halves_of(odd, axis)
        real = jnp.concatenate([er, o_r], axis)
        imag = jnp.concatenate([ei, oi], axis)
    return real, imag


def inverse(real, imag, table):
    for axis in (1, 0):
        (er, o_r), (ei, oi) = halves_of(real, axis), halves_of(imag, axis)
        even = times(jnp.concatenate([er, ei], axis), table, 2, axis)
        odd = times(jnp.concatenate([o_r, oi], axis), table, 3, axis)
        (r0, i0), (r1, i1) = halves_of(even + odd, axis), halves_of(even - odd, axis)
        real = jnp.concatenate([r0, r1], axis)
        imag = jnp.concatenate([i0, i1], axis)
    return real, imag


def amplitude(meas, f, order):
    root = jnp.sqrt(meas[f])
    for axis in (1, 0):
        both = jnp.concatenate(split(root), axis)
        twice = jnp.concatenate([order[1 - axis]] * 2, 1 - axis)
        pair = (both, twice) if axis == 1 else (twice, both)
        root = jnp.dot(*pair, preferred_element_type=jnp.float32)
    return root


def step_kernel(
    pos, wts, obj, probes, meas, table, order, new_obj, q, e, patch, psi, hacc, light, grad, power
):
    waves = probes.shape[0]
    count = meas.shape[0]
    psize = probes.shape[-1]
    side = obj.shape[-1]
    tall = psize + 8
    total = wts[0]
    for w in range(1, waves):
        total = total + wts[w]
    inv_total = 1.0 / jnp.full((1, psize), total)
    light[...] = probes[0, 0] * probes[0, 0] + probes[0, 1] * probes[0, 1]

    def each_wave(start, body):
        if waves - start <= 2:
            for w in range(start, waves):
                body(w)
        else:
            pl.loop(start, waves)(body)

    def add_light(w):
        light[...] += probes[w, 0] * probes[w, 0] + probes[w, 1] * probes[w, 1]

    each_wave(1, add_light)
    new_obj[...] = jnp.zeros_like(new_obj)
    hacc[...] = jnp.zeros_like(hacc)
    q[...] = jnp.zeros_like(q)
    e[...] = jnp.zeros_like(e)

    @pl.loop(0, count)
    def _(f):
        r, c = pos[f, 0], pos[f, 1]
        back = lax.rem(side - c, side)
        base = pl.multiple_of(jnp.minimum(r // 8 * 8, side - tall), 8)
        shift = r - base
        for ch in range(2):
            rows = pltpu.roll(obj[ch, pl.ds(base, tall), :], back, 1)[:, :psize]
            patch[ch] = pltpu.roll(rows, lax.rem(tall - shift, tall), 0)[:psize]
        e[...] += patch[0] * patch[0] + patch[1] * patch[1]
        power[...] = jnp.zeros_like(power)

        def far(w):
            pr, pi = probes[w, 0], probes[w, 1]
            o_r, o_i = patch[0], patch[1]
            real, imag = forward(pr * o_r - pi * o_i, pr * o_i + pi * o_r, table)
            psi[w, 0] = real
            psi[w, 1] = imag
            power[...] += wts[w] * (real * real + imag * imag)

        each_wave(0, far)
        power[...] = (
            amplitude(meas, f, order) / jnp.sqrt(power[...] * inv_total + intensity_offset)
            - 1.0
        )
        grad[...] = jnp.zeros_like(grad)

        def near(w):
            factor = power[...]
            real, imag = inverse(psi[w, 0] * factor, psi[w, 1] * factor, table)
            pr, pi = probes[w, 0], probes[w, 1]
            grad[0] += pr * real + pi * imag
            grad[1] += pr * imag - pi * real
            if isinstance(w, int) and w == 0:
                o_r, o_i = patch[0], patch[1]
                q[0] += o_r * real + o_i * imag
                q[1] += o_r * imag - o_i * real

        near(0)
        each_wave(1, near)

        def place(window):
            below = jnp.zeros((tall - psize, psize), jnp.float32)
            window = pltpu.roll(jnp.concatenate([window, below], 0), shift, 0)
            beside = jnp.zeros((tall, side - psize), jnp.float32)
            return pltpu.roll(jnp.concatenate([window, beside], 1), c, 1)

        for ch in range(2):
            new_obj[ch, pl.ds(base, tall), :] += place(grad[ch])
        hacc[pl.ds(base, tall), :] += place(light[...])

    scale = 1.0 / (hacc[...] + damping)
    for ch in range(2):
        new_obj[ch] = obj[ch] + new_obj[ch] * scale


def local(waves, object_field, probes, measured, positions, weights):
    psize = probes.shape[-1]
    side = object_field.shape[-1]
    table, order = tables(psize)
    all_probes, all_weights = [probes], [weights]
    for turn in range(1, waves):
        ring = [(i, (i + turn) % waves) for i in range(waves)]
        all_probes.append(lax.ppermute(probes, "wave", ring))
        all_weights.append(lax.ppermute(weights, "wave", ring))
    all_probes = jnp.concatenate(all_probes)
    all_weights = jnp.concatenate(all_weights)
    vmem = pl.BlockSpec(memory_space=pltpu.VMEM)
    smem = pl.BlockSpec(memory_space=pltpu.SMEM)
    f32 = jnp.float32
    new_object, q, e = pl.pallas_call(
        step_kernel,
        out_shape=(
            jax.ShapeDtypeStruct(object_field.shape, f32),
            jax.ShapeDtypeStruct((2, psize, psize), f32),
            jax.ShapeDtypeStruct((psize, psize), f32),
        ),
        in_specs=[smem, smem] + [vmem] * 5,
        out_specs=(vmem,) * 3,
        scratch_shapes=[
            pltpu.VMEM((2, psize, psize), f32),
            pltpu.VMEM((waves, 2, psize, psize), f32),
            pltpu.VMEM((side, side), f32),
            pltpu.VMEM((psize, psize), f32),
            pltpu.VMEM((2, psize, psize), f32),
            pltpu.VMEM((psize, psize), f32),
        ],
        compiler_params=pltpu.CompilerParams(vmem_limit_bytes=60 * 2**20),
    )(positions[0, 0], all_weights, object_field, all_probes, measured[0, 0], table, order)
    q, e = lax.psum((q, e), ("ty", "tx"))
    new_probes = probes + (q / (e + damping))[None]
    return (new_object, new_probes)


def at(pos, f, side, tall):
    r, c = pos[f, 0], pos[f, 1]
    base = pl.multiple_of(jnp.minimum(r // 8 * 8, side - tall), 8)
    return base, r - base, c


def raise_rows(rows, shift):
    rows = rows.reshape(-1, 8, rows.shape[-1])
    rows = pltpu.roll(rows, lax.rem(8 - shift, 8), 1)
    within = lax.broadcasted_iota(jnp.int32, rows[1:].shape, 1)
    rows = jnp.where(within < 8 - shift, rows[:-1], rows[1:])
    return rows.reshape(-1, rows.shape[-1])


def lower_rows(rows, shift):
    rows = rows.reshape(-1, 8, rows.shape[-1])
    rows = pltpu.roll(rows, lax.rem(shift, 8), 1)
    none = jnp.zeros((1,) + rows.shape[1:], rows.dtype)
    below, above = jnp.concatenate([rows, none], 0), jnp.concatenate([none, rows], 0)
    within = lax.broadcasted_iota(jnp.int32, below.shape, 1)
    rows = jnp.where(within >= shift, below, above)
    return rows.reshape(-1, rows.shape[-1])


def window_kernel(pos, obj, patch, e):
    psize, side = patch.shape[-1], obj.shape[-1]
    tall = psize + 8
    f = pl.program_id(0)
    base, shift, c = at(pos, f, side, tall)
    power = jnp.zeros((psize, psize), jnp.float32)
    for ch in range(2):
        rows = pltpu.roll(obj[ch, pl.ds(base, tall), :], lax.rem(side - c, side), 1)[:, :psize]
        rows = raise_rows(rows, shift)
        patch[0, ch] = rows
        power += rows * rows

    @pl.when(f == 0)
    def _():
        e[0] = power

    @pl.when(f > 0)
    def _():
        e[0] += power


def scatter_kernel(pos, obj, grad, light, new_obj, hacc):
    psize, side = grad.shape[-1], obj.shape[-1]
    tall = psize + 8
    f = pl.program_id(0)
    base, shift, c = at(pos, f, side, tall)

    @pl.when(f == 0)
    def _():
        new_obj[...] = jnp.zeros_like(new_obj)
        hacc[...] = jnp.zeros_like(hacc)

    def place(window):
        window = lower_rows(window, shift)
        beside = jnp.zeros((tall, side - psize), jnp.float32)
        return pltpu.roll(jnp.concatenate([window, beside], 1), c, 1)

    for ch in range(2):
        new_obj[ch, pl.ds(base, tall), :] += place(grad[0, ch])
    hacc[pl.ds(base, tall), :] += place(light[...])

    @pl.when(f == pl.num_programs(0) - 1)
    def _():
        scale = 1.0 / (hacc[...] + damping)
        for ch in range(2):
            new_obj[ch] = obj[ch] + new_obj[ch] * scale


def pair_kernel(
    bits, rows_of_tiles,
    wts, patch, e, probes, meas, table, order,
    grad, light, new_probes,
    other, wmine, wother, psi, q, q_sums, q_got, e_sums, e_got, q_pieces, e_pieces, result,
    send, recv,
):
    count = meas.shape[0]
    psize = probes.shape[-1]
    f32 = jnp.float32
    wave, ty, tx = lax.axis_index("wave"), lax.axis_index("ty"), lax.axis_index("tx")
    mate = {"wave": 1 - wave}
    halves = []
    for bit in range(bits):
        mine = tx // 2**bit % 2
        halves.append((mine, {"tx": tx + (1 - 2 * mine) * 2**bit}))
    others = [{"ty": lax.rem(ty + d, rows_of_tiles)} for d in range(1, rows_of_tiles)]

    barrier = pltpu.get_barrier_semaphore()
    partners = [mate] + [h[1] for h in halves] + others
    for partner in partners:
        pl.semaphore_signal(
            barrier, inc=1, device_id=partner, device_id_type=pl.DeviceIdType.MESH
        )
    pl.semaphore_wait(barrier, len(partners))

    used = [0]

    def ship(src, dst, partner):
        k = used[0]
        used[0] += 1
        copy = pltpu.make_async_remote_copy(
            src_ref=src, dst_ref=dst, send_sem=send.at[k], recv_sem=recv.at[k],
            device_id=partner, device_id_type=pl.DeviceIdType.MESH,
        )
        copy.start()
        return copy

    wmine[...] = jnp.full(wmine.shape, wts[0], f32)
    core, twin = halves[0]
    strip = pl.ds(pl.multiple_of(core * (psize // 2), 8), psize // 2)
    probe_copies = [
        ship(probes.at[:, :, strip], other.at[:, :, strip], mate),
        ship(wmine, wother, mate),
    ]

    def reduce_rows(source, sums, got, pieces):
        rows = psize
        for step, (mine, partner) in enumerate(halves):
            rows //= 2
            away = pl.ds(pl.multiple_of((1 - mine) * rows, 8), rows)
            copy = ship(source.at[:, away], got[step], partner)
            yield
            copy.wait()
            keep = pl.ds(pl.multiple_of(mine * rows, 8), rows)
            sums[step][...] = source[:, keep] + got[step][...]
            source = sums[step]
        rows //= rows_of_tiles
        copies = []
        for d, partner in enumerate(others):
            away = pl.ds(pl.multiple_of(partner["ty"] * rows, 8), rows)
            copies.append(ship(source.at[:, away], pieces.at[d], partner))
        yield
        for copy in copies:
            copy.wait()
        whole = source[:, pl.ds(pl.multiple_of(ty * rows, 8), rows)]
        for d in range(len(others)):
            whole = whole + pieces[d]
        pieces[len(others)] = whole
        yield

    def spread_rows():
        rows = psize // 2**bits // rows_of_tiles
        first = 0
        height = psize
        for mine, _ in halves:
            height //= 2
            first = first + mine * height
        here = pl.ds(pl.multiple_of(first + ty * rows, 8), rows)
        whole = q_pieces[len(others)] / (e_pieces[len(others)] + damping)
        result[:, here] = probes[0, :, here] + whole
        copies = [ship(result.at[:, here], result.at[:, here], p) for p in others]
        yield
        for copy in copies:
            copy.wait()
        for mine, partner in reversed(halves):
            here = pl.ds(pl.multiple_of(first, 8), height)
            copy = ship(result.at[:, here], result.at[:, here], partner)
            yield
            copy.wait()
            first = first - mine * height
            height *= 2
        yield

    def near(f, side_probes, w):
        pr, pi = side_probes[0, 0], side_probes[0, 1]
        o_r, o_i = patch[f, 0], patch[f, 1]
        real, imag = forward(pr * o_r - pi * o_i, pr * o_i + pi * o_r, table)
        psi[w, f, 0] = real
        psi[w, f, 1] = imag

    def loop(low, high, body):
        if high > low:
            pl.loop(low, high)(body)

    lighting = reduce_rows(e, e_sums, e_got, e_pieces)
    next(lighting)
    loop(0, count, lambda f: near(f, probes, 0))
    for copy in probe_copies:
        copy.wait()
    copy = ship(other.at[:, :, strip], other.at[:, :, strip], twin)
    next(lighting)
    copy.wait()

    w_0, w_1 = wmine[0:1, 0:1], wother[0:1, 0:1]
    total = w_0 + w_1
    w_0, w_1 = w_0 / total, w_1 / total
    light[...] = (
        probes[0, 0] * probes[0, 0] + probes[0, 1] * probes[0, 1]
        + other[0, 0] * other[0, 0] + other[0, 1] * other[0, 1]
    )

    def both(f):
        near(f, other, 1)
        power = w_0 * (psi[0, f, 0] * psi[0, f, 0] + psi[0, f, 1] * psi[0, f, 1])
        power += w_1 * (psi[1, f, 0] * psi[1, f, 0] + psi[1, f, 1] * psi[1, f, 1])
        factor = amplitude(meas, f, order) / jnp.sqrt(power + intensity_offset) - 1.0
        for w in range(2):
            for ch in range(2):
                psi[w, f, ch] *= factor

    marks = [count * i // bits for i in range(bits + 1)]
    for low, high in zip(marks, marks[1:]):
        loop(low, high, both)
        next(lighting)
    q[...] = jnp.zeros_like(q)

    def own(f):
        real, imag = inverse(psi[0, f, 0], psi[0, f, 1], table)
        pr, pi = probes[0, 0], probes[0, 1]
        o_r, o_i = patch[f, 0], patch[f, 1]
        grad[f, 0] = pr * real + pi * imag
        grad[f, 1] = pr * imag - pi * real
        q[0] += o_r * real + o_i * imag
        q[1] += o_r * imag - o_i * real

    loop(0, count, own)

    def rest(f):
        real, imag = inverse(psi[1, f, 0], psi[1, f, 1], table)
        pr, pi = other[0, 0], other[0, 1]
        grad[f, 0] += pr * real + pi * imag
        grad[f, 1] += pr * imag - pi * real

    gather = reduce_rows(q, q_sums, q_got, q_pieces)
    phases = 2 * (bits + 1)
    done = 0

    def work(phase):
        nonlocal done
        later = 1 + (count - 1) * phase // (phases - 2) if phase else 1
        loop(done, min(later, count), rest)
        done = min(later, count)

    for phase in range(bits + 1):
        next(gather)
        work(phase)
    next(gather)
    out = spread_rows()
    next(out)
    for phase in range(bits + 1, phases):
        work(phase)
        next(out)
    new_probes[0] = result[...]


def pair_step(bits, rows_of_tiles, object_field, probes, measured, positions, weights):
    psize = probes.shape[-1]
    side = object_field.shape[-1]
    count = measured.shape[2]
    table, order = tables(psize)
    f32 = jnp.float32
    steps = bits + rows_of_tiles - 1
    copies = 3 + 3 * steps

    def buffers(planes):
        heights = [psize // 2 ** (b + 1) for b in range(bits)]
        halves = [pltpu.VMEM((planes, h, psize), f32) for h in heights]
        return halves

    def pieces(planes):
        rows = psize // 2**bits // rows_of_tiles
        return pltpu.VMEM((rows_of_tiles, planes, rows, psize), f32)

    vmem = pl.BlockSpec(memory_space=pltpu.VMEM)
    smem = pl.BlockSpec(memory_space=pltpu.SMEM)
    one_frame = pl.BlockSpec((1, 2, psize, psize), lambda f: (f, 0, 0, 0))
    frames = jax.ShapeDtypeStruct((count, 2, psize, psize), f32)
    image = jax.ShapeDtypeStruct((1, psize, psize), f32)
    room = pltpu.CompilerParams(vmem_limit_bytes=60 * 2**20)
    patches, e = pl.pallas_call(
        window_kernel,
        grid=(count,),
        out_shape=(frames, image),
        in_specs=[smem, vmem],
        out_specs=(one_frame, vmem),
        compiler_params=room,
    )(positions[0, 0], object_field)
    grad, light, new_probes = pl.pallas_call(
        functools.partial(pair_kernel, bits, rows_of_tiles),
        out_shape=(
            frames,
            jax.ShapeDtypeStruct((psize, psize), f32),
            jax.ShapeDtypeStruct(probes.shape, f32),
        ),
        in_specs=[smem] + [vmem] * 6,
        out_specs=(vmem,) * 3,
        scratch_shapes=[
            pltpu.VMEM(probes.shape, f32),
            pltpu.VMEM((8, 128), f32),
            pltpu.VMEM((8, 128), f32),
            pltpu.VMEM((2, count, 2, psize, psize), f32),
            pltpu.VMEM((2, psize, psize), f32),
            buffers(2),
            buffers(2),
            buffers(1),
            buffers(1),
            pieces(2),
            pieces(1),
            pltpu.VMEM((2, psize, psize), f32),
            pltpu.SemaphoreType.DMA((copies,)),
            pltpu.SemaphoreType.DMA((copies,)),
        ],
        compiler_params=pltpu.CompilerParams(
            vmem_limit_bytes=60 * 2**20, collective_id=0, has_side_effects=True
        ),
    )(weights, patches, e, probes, measured[0, 0], table, order)
    new_object = pl.pallas_call(
        scatter_kernel,
        grid=(count,),
        out_shape=jax.ShapeDtypeStruct(object_field.shape, f32),
        in_specs=[smem, vmem, one_frame, vmem],
        out_specs=vmem,
        scratch_shapes=[pltpu.VMEM((side, side), f32)],
        compiler_params=room,
    )(positions[0, 0], object_field, grad, light)
    return (new_object, new_probes)


def solution(mesh):
    in_specs = (
        P(None, "ty", "tx"),
        P("wave", None, None, None),
        P("ty", "tx", None, None, None),
        P("ty", "tx", None, None),
        P("wave"),
    )
    out_specs = (P(None, "ty", "tx"), P("wave", None, None, None))
    waves, rows_of_tiles, tiles = (mesh.shape[axis] for axis in ("wave", "ty", "tx"))
    bits = tiles.bit_length() - 1
    if waves == 2 and rows_of_tiles > 1 and bits >= 1 and 2**bits == tiles:
        body = functools.partial(pair_step, bits, rows_of_tiles)
    else:
        body = functools.partial(local, waves)
    return jax.shard_map(body, mesh=mesh, in_specs=in_specs, out_specs=out_specs, check_vma=False)
```

```python
import functools
import math

import jax
import jax.numpy as jnp
import numpy as np
from jax import lax
from jax.experimental import pallas as pl
from jax.experimental.pallas import tpu as pltpu
from jax.sharding import PartitionSpec as P

damping = 1.0
intensity_offset = 0.1


def tables(length):
    indices = np.arange(length)
    angles = 2.0 * math.pi / length * (indices[:, None] * indices[None, :] % length)
    cosine = np.cos(angles) / math.sqrt(length)
    sine = -np.sin(angles) / math.sqrt(length)
    half = length // 2
    parts = []
    for odd in range(2):
        c, s = cosine[:half, odd::2], sine[:half, odd::2]
        parts.append(np.block([[c, s], [-s, c]]))
    both = []
    for table in parts + [part.T for part in parts]:
        high = table.astype(jnp.bfloat16)
        low = (table - high.astype(np.float64)).astype(jnp.bfloat16)
        both.append(np.stack([high, low]))
    order = np.concatenate([indices[0::2], indices[1::2]])
    shuffle = (indices[:, None] == order[None, :]).astype(jnp.bfloat16)
    return np.stack(both), np.stack([shuffle, shuffle.T])


def split(x):
    high = x.astype(jnp.bfloat16)
    low = (x - high.astype(jnp.float32)).astype(jnp.bfloat16)
    return high, low


def times(x, table, which, axis):
    high, low = split(x)
    x = jnp.concatenate([high, low, high], axis=axis)
    which = which if axis == 1 else (which + 2) % 4
    high, low = table[which, 0], table[which, 1]
    table = jnp.concatenate([high, high, low], axis=1 - axis)
    pair = (x, table) if axis == 1 else (table, x)
    return jnp.dot(*pair, preferred_element_type=jnp.float32)


def halves_of(x, axis):
    half = x.shape[axis] // 2
    return (x[:, :half], x[:, half:]) if axis == 1 else (x[:half], x[half:])


def forward(real, imag, table):
    for axis in (1, 0):
        (r0, r1), (i0, i1) = halves_of(real, axis), halves_of(imag, axis)
        even = times(jnp.concatenate([r0 + r1, i0 + i1], axis), table, 0, axis)
        odd = times(jnp.concatenate([r0 - r1, i0 - i1], axis), table, 1, axis)
        (er, ei), (o_r, oi) = halves_of(even, axis), halves_of(odd, axis)
        real = jnp.concatenate([er, o_r], axis)
        imag = jnp.concatenate([ei, oi], axis)
    return real, imag


def inverse(real, imag, table):
    for axis in (1, 0):
        (er, o_r), (ei, oi) = halves_of(real, axis), halves_of(imag, axis)
        even = times(jnp.concatenate([er, ei], axis), table, 2, axis)
        odd = times(jnp.concatenate([o_r, oi], axis), table, 3, axis)
        (r0, i0), (r1, i1) = halves_of(even + odd, axis), halves_of(even - odd, axis)
        real = jnp.concatenate([r0, r1], axis)
        imag = jnp.concatenate([i0, i1], axis)
    return real, imag


def amplitude(meas, f, order):
    root = jnp.sqrt(meas[f])
    for axis in (1, 0):
        both = jnp.concatenate(split(root), axis)
        twice = jnp.concatenate([order[1 - axis]] * 2, 1 - axis)
        pair = (both, twice) if axis == 1 else (twice, both)
        root = jnp.dot(*pair, preferred_element_type=jnp.float32)
    return root


def step_kernel(
    pos, wts, obj, probes, meas, table, order, new_obj, q, e, patch, psi, hacc, light, grad, power
):
    waves = probes.shape[0]
    count = meas.shape[0]
    psize = probes.shape[-1]
    side = obj.shape[-1]
    tall = psize + 8
    total = wts[0]
    for w in range(1, waves):
        total = total + wts[w]
    inv_total = 1.0 / jnp.full((1, psize), total)
    light[...] = probes[0, 0] * probes[0, 0] + probes[0, 1] * probes[0, 1]

    def each_wave(start, body):
        if waves - start <= 2:
            for w in range(start, waves):
                body(w)
        else:
            pl.loop(start, waves)(body)

    def add_light(w):
        light[...] += probes[w, 0] * probes[w, 0] + probes[w, 1] * probes[w, 1]

    each_wave(1, add_light)
    new_obj[...] = jnp.zeros_like(new_obj)
    hacc[...] = jnp.zeros_like(hacc)
    q[...] = jnp.zeros_like(q)
    e[...] = jnp.zeros_like(e)

    @pl.loop(0, count)
    def _(f):
        r, c = pos[f, 0], pos[f, 1]
        back = lax.rem(side - c, side)
        base = pl.multiple_of(jnp.minimum(r // 8 * 8, side - tall), 8)
        shift = r - base
        for ch in range(2):
            rows = pltpu.roll(obj[ch, pl.ds(base, tall), :], back, 1)[:, :psize]
            patch[ch] = pltpu.roll(rows, lax.rem(tall - shift, tall), 0)[:psize]
        e[...] += patch[0] * patch[0] + patch[1] * patch[1]
        power[...] = jnp.zeros_like(power)

        def far(w):
            pr, pi = probes[w, 0], probes[w, 1]
            o_r, o_i = patch[0], patch[1]
            real, imag = forward(pr * o_r - pi * o_i, pr * o_i + pi * o_r, table)
            psi[w, 0] = real
            psi[w, 1] = imag
            power[...] += wts[w] * (real * real + imag * imag)

        each_wave(0, far)
        power[...] = (
            amplitude(meas, f, order) / jnp.sqrt(power[...] * inv_total + intensity_offset)
            - 1.0
        )
        grad[...] = jnp.zeros_like(grad)

        def near(w):
            factor = power[...]
            real, imag = inverse(psi[w, 0] * factor, psi[w, 1] * factor, table)
            pr, pi = probes[w, 0], probes[w, 1]
            grad[0] += pr * real + pi * imag
            grad[1] += pr * imag - pi * real
            if isinstance(w, int) and w == 0:
                o_r, o_i = patch[0], patch[1]
                q[0] += o_r * real + o_i * imag
                q[1] += o_r * imag - o_i * real

        near(0)
        each_wave(1, near)

        def place(window):
            below = jnp.zeros((tall - psize, psize), jnp.float32)
            window = pltpu.roll(jnp.concatenate([window, below], 0), shift, 0)
            beside = jnp.zeros((tall, side - psize), jnp.float32)
            return pltpu.roll(jnp.concatenate([window, beside], 1), c, 1)

        for ch in range(2):
            new_obj[ch, pl.ds(base, tall), :] += place(grad[ch])
        hacc[pl.ds(base, tall), :] += place(light[...])

    scale = 1.0 / (hacc[...] + damping)
    for ch in range(2):
        new_obj[ch] = obj[ch] + new_obj[ch] * scale


def local(waves, object_field, probes, measured, positions, weights):
    psize = probes.shape[-1]
    side = object_field.shape[-1]
    table, order = tables(psize)
    all_probes, all_weights = [probes], [weights]
    for turn in range(1, waves):
        ring = [(i, (i + turn) % waves) for i in range(waves)]
        all_probes.append(lax.ppermute(probes, "wave", ring))
        all_weights.append(lax.ppermute(weights, "wave", ring))
    all_probes = jnp.concatenate(all_probes)
    all_weights = jnp.concatenate(all_weights)
    vmem = pl.BlockSpec(memory_space=pltpu.VMEM)
    smem = pl.BlockSpec(memory_space=pltpu.SMEM)
    f32 = jnp.float32
    new_object, q, e = pl.pallas_call(
        step_kernel,
        out_shape=(
            jax.ShapeDtypeStruct(object_field.shape, f32),
            jax.ShapeDtypeStruct((2, psize, psize), f32),
            jax.ShapeDtypeStruct((psize, psize), f32),
        ),
        in_specs=[smem, smem] + [vmem] * 5,
        out_specs=(vmem,) * 3,
        scratch_shapes=[
            pltpu.VMEM((2, psize, psize), f32),
            pltpu.VMEM((waves, 2, psize, psize), f32),
            pltpu.VMEM((side, side), f32),
            pltpu.VMEM((psize, psize), f32),
            pltpu.VMEM((2, psize, psize), f32),
            pltpu.VMEM((psize, psize), f32),
        ],
        compiler_params=pltpu.CompilerParams(vmem_limit_bytes=60 * 2**20),
    )(positions[0, 0], all_weights, object_field, all_probes, measured[0, 0], table, order)
    q, e = lax.psum((q, e), ("ty", "tx"))
    new_probes = probes + (q / (e + damping))[None]
    return (new_object, new_probes)


def at(pos, f, side, tall):
    r, c = pos[f, 0], pos[f, 1]
    base = pl.multiple_of(jnp.minimum(r // 8 * 8, side - tall), 8)
    return base, r - base, c


def raise_rows(rows, shift):
    rows = rows.reshape(-1, 8, rows.shape[-1])
    rows = pltpu.roll(rows, lax.rem(8 - shift, 8), 1)
    within = lax.broadcasted_iota(jnp.int32, rows[1:].shape, 1)
    rows = jnp.where(within < 8 - shift, rows[:-1], rows[1:])
    return rows.reshape(-1, rows.shape[-1])


def lower_rows(rows, shift):
    rows = rows.reshape(-1, 8, rows.shape[-1])
    rows = pltpu.roll(rows, lax.rem(shift, 8), 1)
    none = jnp.zeros((1,) + rows.shape[1:], rows.dtype)
    below, above = jnp.concatenate([rows, none], 0), jnp.concatenate([none, rows], 0)
    within = lax.broadcasted_iota(jnp.int32, below.shape, 1)
    rows = jnp.where(within >= shift, below, above)
    return rows.reshape(-1, rows.shape[-1])


def window_kernel(pos, obj, patch, e):
    psize, side = patch.shape[-1], obj.shape[-1]
    tall = psize + 8
    f = pl.program_id(0)
    base, shift, c = at(pos, f, side, tall)
    power = jnp.zeros((psize, psize), jnp.float32)
    for ch in range(2):
        rows = pltpu.roll(obj[ch, pl.ds(base, tall), :], lax.rem(side - c, side), 1)[:, :psize]
        rows = raise_rows(rows, shift)
        patch[0, ch] = rows
        power += rows * rows

    @pl.when(f == 0)
    def _():
        e[0] = power

    @pl.when(f > 0)
    def _():
        e[0] += power


def scatter_kernel(pos, obj, grad, light, new_obj, hacc):
    psize, side = grad.shape[-1], obj.shape[-1]
    tall = psize + 8
    f = pl.program_id(0)
    base, shift, c = at(pos, f, side, tall)

    @pl.when(f == 0)
    def _():
        new_obj[...] = jnp.zeros_like(new_obj)
        hacc[...] = jnp.zeros_like(hacc)

    def place(window):
        window = lower_rows(window, shift)
        beside = jnp.zeros((tall, side - psize), jnp.float32)
        return pltpu.roll(jnp.concatenate([window, beside], 1), c, 1)

    for ch in range(2):
        new_obj[ch, pl.ds(base, tall), :] += place(grad[0, ch])
    hacc[pl.ds(base, tall), :] += place(light[...])

    @pl.when(f == pl.num_programs(0) - 1)
    def _():
        scale = 1.0 / (hacc[...] + damping)
        for ch in range(2):
            new_obj[ch] = obj[ch] + new_obj[ch] * scale


def pair_kernel(
    bits, rows_of_tiles,
    wts, patch, e, probes, meas, table, order,
    grad, light, new_probes,
    other, wmine, wother, psi, q, q_sums, q_got, e_sums, e_got, q_pieces, e_pieces, result,
    send, recv,
):
    count = meas.shape[0]
    psize = probes.shape[-1]
    f32 = jnp.float32
    wave, ty, tx = lax.axis_index("wave"), lax.axis_index("ty"), lax.axis_index("tx")
    mate = {"wave": 1 - wave}
    halves = []
    for bit in range(bits):
        mine = tx // 2**bit % 2
        halves.append((mine, {"tx": tx + (1 - 2 * mine) * 2**bit}))
    others = [{"ty": lax.rem(ty + d, rows_of_tiles)} for d in range(1, rows_of_tiles)]

    barrier = pltpu.get_barrier_semaphore()
    partners = [mate] + [h[1] for h in halves] + others
    for partner in partners:
        pl.semaphore_signal(
            barrier, inc=1, device_id=partner, device_id_type=pl.DeviceIdType.MESH
        )
    pl.semaphore_wait(barrier, len(partners))

    used = [0]

    def ship(src, dst, partner):
        k = used[0]
        used[0] += 1
        copy = pltpu.make_async_remote_copy(
            src_ref=src, dst_ref=dst, send_sem=send.at[k], recv_sem=recv.at[k],
            device_id=partner, device_id_type=pl.DeviceIdType.MESH,
        )
        copy.start()
        return copy

    wmine[...] = jnp.full(wmine.shape, wts[0], f32)
    core, twin = halves[0]
    strip = pl.ds(pl.multiple_of(core * (psize // 2), 8), psize // 2)
    probe_copies = [
        ship(probes.at[:, :, strip], other.at[:, :, strip], mate),
        ship(wmine, wother, mate),
    ]

    def reduce_rows(source, sums, got, pieces):
        rows = psize
        for step, (mine, partner) in enumerate(halves):
            rows //= 2
            away = pl.ds(pl.multiple_of((1 - mine) * rows, 8), rows)
            copy = ship(source.at[:, away], got[step], partner)
            yield
            copy.wait()
            keep = pl.ds(pl.multiple_of(mine * rows, 8), rows)
            sums[step][...] = source[:, keep] + got[step][...]
            source = sums[step]
        rows //= rows_of_tiles
        copies = []
        for d, partner in enumerate(others):
            away = pl.ds(pl.multiple_of(partner["ty"] * rows, 8), rows)
            copies.append(ship(source.at[:, away], pieces.at[d], partner))
        yield
        for copy in copies:
            copy.wait()
        whole = source[:, pl.ds(pl.multiple_of(ty * rows, 8), rows)]
        for d in range(len(others)):
            whole = whole + pieces[d]
        pieces[len(others)] = whole
        yield

    def spread_rows():
        rows = psize // 2**bits // rows_of_tiles
        first = 0
        height = psize
        for mine, _ in halves:
            height //= 2
            first = first + mine * height
        here = pl.ds(pl.multiple_of(first + ty * rows, 8), rows)
        whole = q_pieces[len(others)] / (e_pieces[len(others)] + damping)
        result[:, here] = probes[0, :, here] + whole
        copies = [ship(result.at[:, here], result.at[:, here], p) for p in others]
        yield
        for copy in copies:
            copy.wait()
        for mine, partner in reversed(halves):
            here = pl.ds(pl.multiple_of(first, 8), height)
            copy = ship(result.at[:, here], result.at[:, here], partner)
            yield
            copy.wait()
            first = first - mine * height
            height *= 2
        yield

    def near(f, side_probes, w):
        pr, pi = side_probes[0, 0], side_probes[0, 1]
        o_r, o_i = patch[f, 0], patch[f, 1]
        real, imag = forward(pr * o_r - pi * o_i, pr * o_i + pi * o_r, table)
        psi[w, f, 0] = real
        psi[w, f, 1] = imag

    def loop(low, high, body):
        if high > low:
            pl.loop(low, high)(body)

    lighting = reduce_rows(e, e_sums, e_got, e_pieces)
    next(lighting)
    loop(0, count, lambda f: near(f, probes, 0))
    for copy in probe_copies:
        copy.wait()
    copy = ship(other.at[:, :, strip], other.at[:, :, strip], twin)
    next(lighting)
    copy.wait()

    w_0, w_1 = wmine[0:1, 0:1], wother[0:1, 0:1]
    total = w_0 + w_1
    w_0, w_1 = w_0 / total, w_1 / total
    light[...] = (
        probes[0, 0] * probes[0, 0] + probes[0, 1] * probes[0, 1]
        + other[0, 0] * other[0, 0] + other[0, 1] * other[0, 1]
    )

    def both(f):
        near(f, other, 1)
        power = w_0 * (psi[0, f, 0] * psi[0, f, 0] + psi[0, f, 1] * psi[0, f, 1])
        power += w_1 * (psi[1, f, 0] * psi[1, f, 0] + psi[1, f, 1] * psi[1, f, 1])
        factor = amplitude(meas, f, order) / jnp.sqrt(power + intensity_offset) - 1.0
        for w in range(2):
            for ch in range(2):
                psi[w, f, ch] *= factor

    marks = [count * i // bits for i in range(bits + 1)]
    for low, high in zip(marks, marks[1:]):
        loop(low, high, both)
        next(lighting)
    q[...] = jnp.zeros_like(q)

    def own(f):
        real, imag = inverse(psi[0, f, 0], psi[0, f, 1], table)
        pr, pi = probes[0, 0], probes[0, 1]
        o_r, o_i = patch[f, 0], patch[f, 1]
        grad[f, 0] = pr * real + pi * imag
        grad[f, 1] = pr * imag - pi * real
        q[0] += o_r * real + o_i * imag
        q[1] += o_r * imag - o_i * real

    loop(0, count, own)

    def rest(f):
        real, imag = inverse(psi[1, f, 0], psi[1, f, 1], table)
        pr, pi = other[0, 0], other[0, 1]
        grad[f, 0] += pr * real + pi * imag
        grad[f, 1] += pr * imag - pi * real

    gather = reduce_rows(q, q_sums, q_got, q_pieces)
    phases = 2 * (bits + 1)
    done = 0

    def work(phase):
        nonlocal done
        later = 1 + (count - 1) * phase // (phases - 2) if phase else 1
        loop(done, min(later, count), rest)
        done = min(later, count)

    for phase in range(bits + 1):
        next(gather)
        work(phase)
    next(gather)
    out = spread_rows()
    next(out)
    for phase in range(bits + 1, phases):
        work(phase)
        next(out)
    new_probes[0] = result[...]


def pair_step(bits, rows_of_tiles, object_field, probes, measured, positions, weights):
    psize = probes.shape[-1]
    side = object_field.shape[-1]
    count = measured.shape[2]
    table, order = tables(psize)
    f32 = jnp.float32
    steps = bits + rows_of_tiles - 1
    copies = 3 + 3 * steps

    def buffers(planes):
        heights = [psize // 2 ** (b + 1) for b in range(bits)]
        halves = [pltpu.VMEM((planes, h, psize), f32) for h in heights]
        return halves

    def pieces(planes):
        rows = psize // 2**bits // rows_of_tiles
        return pltpu.VMEM((rows_of_tiles, planes, rows, psize), f32)

    vmem = pl.BlockSpec(memory_space=pltpu.VMEM)
    smem = pl.BlockSpec(memory_space=pltpu.SMEM)
    one_frame = pl.BlockSpec((1, 2, psize, psize), lambda f: (f, 0, 0, 0))
    frames = jax.ShapeDtypeStruct((count, 2, psize, psize), f32)
    image = jax.ShapeDtypeStruct((1, psize, psize), f32)
    room = pltpu.CompilerParams(vmem_limit_bytes=20 * 2**20)
    patches, e = pl.pallas_call(
        window_kernel,
        grid=(count,),
        out_shape=(frames, image),
        in_specs=[smem, vmem],
        out_specs=(one_frame, vmem),
        compiler_params=room,
    )(positions[0, 0], object_field)
    grad, light, new_probes = pl.pallas_call(
        functools.partial(pair_kernel, bits, rows_of_tiles),
        out_shape=(
            frames,
            jax.ShapeDtypeStruct((psize, psize), f32),
            jax.ShapeDtypeStruct(probes.shape, f32),
        ),
        in_specs=[smem] + [vmem] * 6,
        out_specs=(vmem,) * 3,
        scratch_shapes=[
            pltpu.VMEM(probes.shape, f32),
            pltpu.VMEM((8, 128), f32),
            pltpu.VMEM((8, 128), f32),
            pltpu.VMEM((2, count, 2, psize, psize), f32),
            pltpu.VMEM((2, psize, psize), f32),
            buffers(2),
            buffers(2),
            buffers(1),
            buffers(1),
            pieces(2),
            pieces(1),
            pltpu.VMEM((2, psize, psize), f32),
            pltpu.SemaphoreType.DMA((copies,)),
            pltpu.SemaphoreType.DMA((copies,)),
        ],
        compiler_params=pltpu.CompilerParams(
            vmem_limit_bytes=40 * 2**20, collective_id=0, has_side_effects=True
        ),
    )(weights, patches, e, probes, measured[0, 0], table, order)
    new_object = pl.pallas_call(
        scatter_kernel,
        grid=(count,),
        out_shape=jax.ShapeDtypeStruct(object_field.shape, f32),
        in_specs=[smem, vmem, one_frame, vmem],
        out_specs=vmem,
        scratch_shapes=[pltpu.VMEM((side, side), f32)],
        compiler_params=room,
    )(positions[0, 0], object_field, grad, light)
    return (new_object, new_probes)


def solution(mesh):
    in_specs = (
        P(None, "ty", "tx"),
        P("wave", None, None, None),
        P("ty", "tx", None, None, None),
        P("ty", "tx", None, None),
        P("wave"),
    )
    out_specs = (P(None, "ty", "tx"), P("wave", None, None, None))
    waves, rows_of_tiles, tiles = (mesh.shape[axis] for axis in ("wave", "ty", "tx"))
    bits = tiles.bit_length() - 1
    if waves == 2 and rows_of_tiles > 1 and bits >= 1 and 2**bits == tiles:
        body = functools.partial(pair_step, bits, rows_of_tiles)
    else:
        body = functools.partial(local, waves)
    return jax.shard_map(body, mesh=mesh, in_specs=in_specs, out_specs=out_specs, check_vma=False)
```
